128 devices in a mesh: sect: 2 (over core), grp: 8 (over x, z_hi), dev: 8 (over z_lo, y).
Axes of the slice: x: 4, y: 4, z: 4 (z_hi: 2, z_lo: 2; z = z_hi * 2 + z_lo), core: 2. Of those that a mesh axis runs over, the one named last changes fastest.
Arguments:
- tokens: bfloat16 [512, 7168], P(('sect', 'grp', 'dev')), may hold values from -6 to 6
- expert_ids: int32 [512, 8], P(('sect', 'grp', 'dev')), may hold values from 0 to 31, all different within a row; in each aligned block of 4 rows (0 to 3, 4 to 7, ...) at most 2 rows name the same one
- gate_weights: float32 [512, 8], P(('sect', 'grp', 'dev')), may hold values from 0.1 to 0.6
- w_gate: bfloat16 [32, 7168, 2048], P(('sect', 'grp'), None, 'dev'), may hold values from -0.0625 to 0.0625
- w_up: bfloat16 [32, 7168, 2048], P(('sect', 'grp'), None, 'dev'), may hold values from -0.0625 to 0.0625
- w_down: bfloat16 [32, 2048, 7168], P(('sect', 'grp'), 'dev'), may hold values from -0.125 to 0.125
Outputs:
- mixed: bfloat16 [512, 7168], P(('sect', 'grp', 'dev'))
The draws below stay inside these ranges and needn't reach their ends.
Inputs may be any that keep to these rules, and one draw needn't show every extreme that they name: `expert_ids`: each row names 8 different experts. Within the 4 rows of one device no expert is named by more than 2 rows, and on some device some expert is named by exactly 2.
All inputs are finite; a program needn't handle non-finite values.
Results may differ from the reference program's by a relative error of at most 0.015.
Values may be sent and summed in bfloat16 or wider, within the bound.
A program may use at most 128 MiB of HBM per device.

```python
import math
import jax
import jax.numpy as jnp
import numpy as np
from jax import lax

D = 7168
FF = 2048
TOP = 8
TOK_DEV = 4
CAP = 2
EXPERTS = 32
FF_DEV = 256
TOKENS = 512


def shard_levels(stream_key, shape, shards, least, top_value):
    def one(position, shards_of):
        heights = jax.random.uniform(jax.random.fold_in(jax.random.fold_in(stream_key, 6), position), (shards_of,), jnp.float32, least / len(shards), top_value / len(shards))
        return jnp.repeat(jnp.exp(heights), shape[position] // shards_of).reshape((-1,) + (1,) * (len(shape) - position - 1))

    factor_of = one(*shards[0])
    for cut in shards[1:]:
        factor_of = factor_of * one(*cut)
    return factor_of


def deal_out(own_key, own, number, rows, count, top, limit, slope):
    order = jax.random.permutation(own_key, count)
    crowded, ordinary = portions_of(count, rows * top, limit, slope, True), portions_of(count, rows * top, limit, slope, False)
    places = jnp.arange(count)

    def named(tallies, offset_by):
        used = int((tallies > 0).sum())
        fixed = max(1, used // 4)
        passed = fixed + (places - fixed + offset_by * (used - fixed)) % max(1, count - fixed)
        return jnp.zeros((count,), jnp.int32).at[order[jnp.where(places < fixed, places, passed)]].set(jnp.asarray(tallies, jnp.int32))

    tallies = jnp.where(number % 4 == 0, named(crowded, number // 4), named(ordinary, number - number // 4 - 1))
    mixed = jax.random.permutation(jax.random.fold_in(own, 3), count)
    source_of, sink = mixed[0:count // 2 * 2:2], mixed[1:count // 2 * 2:2]
    room = jnp.minimum(tallies[source_of] - 1, limit - tallies[sink]) // 2
    room = jnp.where((source_of == order[0]) | (sink == order[0]) | (tallies[sink] == 0), 0, jnp.maximum(room, 0))
    passed = jax.random.randint(jax.random.fold_in(own, 4), (count // 2,), 0, 1 << 20) % (room + 1)
    tallies = tallies.at[source_of].add(-passed).at[sink].add(passed)
    items = jnp.searchsorted(jnp.cumsum(tallies), jnp.arange(rows * top), side="right").astype(jnp.int32)
    listing = items.reshape(top, rows).T
    listing = listing[jax.random.permutation(jax.random.fold_in(own, 1), rows)]
    offset_by = jax.random.randint(jax.random.fold_in(own, 2), (rows, 1), 0, top)
    return jnp.take_along_axis(listing, (jnp.arange(top)[None, :] + offset_by) % top, axis=1)


def portions_of(number_of, total, limit, lean, full):
    loads = [(1 << 20) // math.isqrt(rank ** lean) + 1 for rank in range(1, number_of + 1)]
    largest = limit if full else min(limit, max(-(-total // number_of), total * loads[0] // sum(loads)))
    least = 1 if total - largest >= number_of - 1 else 0
    counts, rest = [largest] + [least] * (number_of - 1), total - largest - least * (number_of - 1)
    while rest > 0:
        candidates = [i for i in range(1, number_of) if counts[i] < largest] or [i for i in range(1, number_of) if counts[i] < limit]
        whole, remaining = sum([loads[i] for i in candidates]), rest
        for i in candidates:
            extra = min(limit - counts[i], max(1, remaining * loads[i] // whole), rest)
            counts[i] = counts[i] + extra
            rest = rest - extra
    return np.array(counts)


def scatter_about(key, extent, spread, bound, split=(), kind=jnp.bfloat16):
    factor_of = shard_levels(key, extent, split, -0.22, 0.18) if split else 1.0
    drawn = jax.random.normal(key, extent, jnp.float32) * spread * factor_of
    return jnp.minimum(jnp.maximum(drawn, -bound), bound).astype(kind)


def setup_inputs(seed: int = 0) -> dict:
    seeds = jax.random.split(jax.random.key(seed), 7)
    tokens = scatter_about(seeds[0], (TOKENS, D), 1.0, 6.0, ((0, 128),))
    expert_ids_keys = jax.random.split(jax.random.fold_in(seeds[1], 1), TOKENS // TOK_DEV)
    expert_ids_turns = jax.random.permutation(jax.random.fold_in(seeds[1], 3), TOKENS // TOK_DEV)
    expert_ids = jax.vmap(lambda own, number: deal_out(jax.random.fold_in(seeds[1], 2), own, number, TOK_DEV, EXPERTS, TOP, CAP, 2))(expert_ids_keys, expert_ids_turns).reshape((TOKENS, TOP))
    gate_weights = jnp.clip(0.1 + 0.5 * jax.random.uniform(seeds[2], (TOKENS, TOP), jnp.float32) ** shard_levels(seeds[2], (TOKENS, TOP), ((0, 128),), -0.2, 0.2), 0.1, 0.6)
    w_gate = scatter_about(seeds[3], (EXPERTS, D, FF), D ** -0.5, 0.0625, ((0, 16), (2, 8)))
    w_up = scatter_about(seeds[4], (EXPERTS, D, FF), D ** -0.5, 0.0625, ((0, 16), (2, 8)))
    w_down = scatter_about(seeds[5], (EXPERTS, FF, D), FF ** -0.5, 0.125, ((0, 16), (1, 8)))
    return {"tokens": tokens, "expert_ids": expert_ids, "gate_weights": gate_weights, "w_gate": w_gate, "w_up": w_up, "w_down": w_down}


def reference(tokens, expert_ids, gate_weights, w_gate, w_up, w_down):
    buffer_rows = (TOKENS // TOK_DEV) * CAP
    blocks = FF // FF_DEV

    def one_expert(running, expert_index):
        naming = expert_ids == expert_index
        chosen = jnp.any(naming, axis=1)
        weight = jnp.sum(jnp.where(naming, gate_weights, 0.0), axis=1)
        picked = jnp.nonzero(chosen, size=buffer_rows, fill_value=0)[0].astype(jnp.int32)
        occupied = jnp.arange(buffer_rows, dtype=jnp.int32) < jnp.sum(chosen.astype(jnp.int32))
        gathered = tokens[picked]
        gate_proj = jnp.dot(gathered, w_gate[expert_index], preferred_element_type=jnp.float32)
        up_proj = jnp.dot(gathered, w_up[expert_index], preferred_element_type=jnp.float32)
        hidden = (jax.nn.silu(gate_proj) * up_proj).astype(jnp.bfloat16)
        down_rows = w_down[expert_index]
        result = jnp.zeros((buffer_rows, D), jnp.float32)
        for block_index in range(blocks):
            lower = block_index * FF_DEV
            block_part = jnp.dot(hidden[:, lower:lower + FF_DEV], down_rows[lower:lower + FF_DEV], preferred_element_type=jnp.float32).astype(jnp.bfloat16)
            result = result + lax.optimization_barrier(block_part).astype(jnp.float32)
        expert_out = lax.optimization_barrier(result.astype(jnp.bfloat16)).astype(jnp.float32)
        row_scale = jnp.where(occupied, weight[picked], 0.0)
        running = running.at[picked].add(row_scale[:, None] * expert_out)
        return running, None

    running, _ = lax.scan(one_expert, jnp.zeros((TOKENS, D), jnp.float32), jnp.arange(EXPERTS, dtype=jnp.int32))
    return running.astype(jnp.bfloat16)
```

```python
import functools

import jax
import jax.numpy as jnp
from jax import lax
from jax.experimental import pallas as pl
from jax.experimental.pallas import tpu as pltpu
from jax.sharding import PartitionSpec as P

ALL = ("sect", "grp", "dev")
MESH = pl.DeviceIdType.MESH
SIDE = 4
LANES = 128
ORDERS = ((0, 1, 2), (1, 2, 0), (2, 0, 1))


def thirds(width):
    tiles = width // LANES
    counts = [tiles // 3 + (1 if i < tiles % 3 else 0) for i in range(3)]
    parts, low = [], 0
    for count in counts:
        cut = low + (count + 1) // 2 * LANES
        high = low + count * LANES
        parts.append((low, cut, high))
        low = high
    return parts


def kernel(half, t8, wg_hbm, wu_hbm, wd_hbm, out, tr, xs, wall, wd, hid, ps, r0, *rest):
    fa, fb, rl, rr, fin = rest[0:9], rest[9:18], rest[18:27], rest[27:36], rest[36]
    wsem, ex_s, ex_r, ag_s, ag_r, dd_s, dd_r, pr_s, pr_r, rs_s, rs_r = rest[37:]
    wide = half + LANES
    experts = wg_hbm.shape[0]
    hidden_width = wg_hbm.shape[2]
    c, g, d = lax.axis_index("sect"), lax.axis_index("grp"), lax.axis_index("dev")
    other = 1 - c
    me = (g // 2, d % SIDE, (g % 2) * 2 + d // SIDE)

    def device(pos, core):
        x, y, z = pos
        return {"sect": core, "grp": x * 2 + z // 2, "dev": (z % 2) * SIDE + y}

    def shifted(axis, by):
        return tuple(lax.rem(m + by, SIDE) if a == axis else m for a, m in enumerate(me))

    twin = device(me, other)
    right = [device(shifted(a, 1), c) for a in range(3)]
    left = [device(shifted(a, SIDE - 1), c) for a in range(3)]

    barrier = pltpu.get_barrier_semaphore()
    for peer in [twin] + right + left:
        pl.semaphore_signal(barrier, inc=1, device_id=peer, device_id_type=MESH)

    weights = []
    for j in range(experts):
        for i, src in enumerate((wg_hbm, wu_hbm)):
            at = (2 * j + i) * hidden_width
            weights.append(
                pltpu.make_async_copy(src.at[j], wall.at[:, at : at + hidden_width], wsem.at[2 * j + i])
            )
    for j in range(experts):
        for h in range(2):
            weights.append(
                pltpu.make_async_copy(
                    wd_hbm.at[j, :, h * half : (h + 1) * half],
                    wd.at[h, j * hidden_width : (j + 1) * hidden_width],
                    wsem.at[2 * experts + 2 * j + h],
                )
            )
    for copy in weights:
        copy.start()
    pl.semaphore_wait(barrier, 7)

    def remote(src, dst, send, recv, peer):
        return pltpu.make_async_remote_copy(
            src_ref=src, dst_ref=dst, send_sem=send, recv_sem=recv, device_id=peer, device_id_type=MESH
        )

    def spot(part, stage, value):
        order = ORDERS[part]
        index = []
        for axis in range(3):
            if axis in order[:stage]:
                index.append(slice(None))
            elif axis == order[stage]:
                index.append(value)
            else:
                index.append(me[axis])
        return tuple(index) + (slice(None),)

    sent = []

    def go(copy):
        copy.start()
        sent.append(copy)

    swap = remote(t8.at[other], tr, ex_s, ex_r, twin)
    swap.start()
    swap.wait()
    xs[(c,) + me] = t8[c] + tr[...]

    ag_parts = thirds(wide)

    def ag(part, stage, kind, value, low, high, peer):
        ref = xs.at[(c,) + spot(part, stage, value) + (slice(low, high),)]
        return remote(ref, ref, ag_s.at[part, stage, kind], ag_r.at[part, stage, kind], peer)

    def across(part, stage, kind, half_index, value):
        low, _, high = ag_parts[part]
        ref = xs.at[(half_index,) + spot(part, stage, value) + (slice(low, high),)]
        return remote(ref, ref, dd_s.at[part, stage, kind], dd_r.at[part, stage, kind], twin)

    for stage in range(3):
        for part in range(3):
            axis = ORDERS[part][stage]
            low, cut, high = ag_parts[part]
            go(ag(part, stage, 0, me[axis], low, high, right[axis]))
            go(ag(part, stage, 1, me[axis], low, high, left[axis]))
            if stage == 0:
                go(across(part, stage, 3, c, me[axis]))
        for part in range(3):
            axis = ORDERS[part][stage]
            low, cut, high = ag_parts[part]
            before, after = shifted(axis, SIDE - 1)[axis], shifted(axis, 1)[axis]
            ag(part, stage, 0, before, low, high, twin).wait_recv()
            go(ag(part, stage, 2, before, low, cut, right[axis]))
            go(across(part, stage, 0, c, before))
            ag(part, stage, 1, after, low, high, twin).wait_recv()
            go(ag(part, stage, 3, after, cut, high, left[axis]))
            go(across(part, stage, 1, c, after))
        for part in range(3):
            axis = ORDERS[part][stage]
            low, cut, high = ag_parts[part]
            far = shifted(axis, 2)[axis]
            ag(part, stage, 2, far, low, cut, twin).wait_recv()
            ag(part, stage, 3, far, cut, high, twin).wait_recv()
            go(across(part, stage, 2, c, far))
    for stage in range(3):
        for part in range(3):
            axis = ORDERS[part][stage]
            for kind, by in ((3, 0), (0, SIDE - 1), (1, 1), (2, 2)):
                if kind < 3 or stage == 0:
                    across(part, stage, kind, other, shifted(axis, by)[axis]).wait_recv()
    for copy in weights:
        copy.wait()

    first = (c * 8 + g) * experts
    row = lax.broadcasted_iota(jnp.int32, (LANES, hidden_width), 0)
    picks = []
    for j in range(experts):
        e = first + j
        hit = (row == e) | (row == e + 32) | (row == e + 64)
        picks.append(jnp.where(hit, 1.0, 0.0).astype(jnp.bfloat16))

    span = 2
    rows = span * SIDE * SIDE * 8

    def up_step(m, carry):
        at = pl.ds(m * span, span)
        v0 = xs[0, at, :, :, :, 0:half].reshape(rows, half)
        v1 = xs[1, at, :, :, :, 0:half].reshape(rows, half)
        share = xs[0, at, :, :, :, half:wide].reshape(rows, LANES)
        for j in range(experts):
            cols = slice(2 * j * hidden_width, (2 * j + 2) * hidden_width)
            both = jnp.dot(v0, wall[0:half, cols], preferred_element_type=jnp.float32)
            both += jnp.dot(v1, wall[half : 2 * half, cols], preferred_element_type=jnp.float32)
            gate, up = both[:, :hidden_width], both[:, hidden_width:]
            weight = jnp.dot(share, picks[j], preferred_element_type=jnp.float32)
            act = gate / (1.0 + jnp.exp(-gate)) * up * weight
            hid[pl.ds(pl.multiple_of(m * rows, rows), rows), j * hidden_width : (j + 1) * hidden_width] = act.astype(
                jnp.bfloat16
            )
        return carry

    lax.fori_loop(0, SIDE // span, up_step, 0)

    rs_parts = thirds(half)

    def down(half_index, part):
        low, _, high = rs_parts[part]

        def step(m, carry):
            value = jnp.dot(
                hid[pl.ds(pl.multiple_of(m * rows, rows), rows), :],
                wd[half_index, :, low:high],
                preferred_element_type=jnp.float32,
            ).astype(jnp.bfloat16)
            ps[half_index, pl.ds(m * span, span), :, :, :, low:high] = value.reshape(
                span, SIDE, SIDE, 8, high - low
            )
            return carry

        lax.fori_loop(0, SIDE // span, step, 0)

    def pair(part, half_index):
        low, _, high = rs_parts[part]
        cols = (slice(None),) * 4 + (slice(low, high),)
        return remote(
            ps.at[(half_index,) + cols], r0.at[cols], pr_s.at[part], pr_r.at[part], twin
        )

    def plus(index, *others):
        total = ps[index].astype(jnp.float32)
        for value in others:
            total += value.astype(jnp.float32)
        ps[index] = total.astype(jnp.bfloat16)

    def rs(part, stage, kind, value, low, high, buf, peer):
        base = rs_parts[part][0]
        ref = ps.at[(c,) + spot(part, stage, value) + (slice(low, high),)]
        dst = buf[part * 3 + stage]
        dst = dst.at[(slice(None),) * (stage + 1) + (slice(low - base, high - base),)] if kind > 1 else dst
        return remote(ref, dst, rs_s.at[part, stage, kind], rs_r.at[part, stage, kind], peer)

    def copy_of(part, stage, kind):
        axis = ORDERS[part][stage]
        low, cut, high = rs_parts[part]
        far, after, before = (shifted(axis, by)[axis] for by in (2, 1, SIDE - 1))
        value, start, stop, buf, peer = (
            (far, low, cut, fa, right),
            (far, cut, high, fb, left),
            (after, cut, high, rl, right),
            (before, low, cut, rr, left),
            (after, low, cut, rl, right),
            (before, cut, high, rr, left),
        )[kind]
        return rs(part, stage, kind, value, start, stop, buf, peer[axis])

    def open_stage(part, stage):
        for kind in range(4):
            go(copy_of(part, stage, kind))

    for part in range(3):
        down(other, part)
        go(pair(part, other))
    for part in range(3):
        down(c, part)
        pair(part, c).wait_recv()
        low, _, high = rs_parts[part]

        def add_pair(i, carry):
            plus((c, i, slice(None), slice(None), slice(None), slice(low, high)), r0[i, :, :, :, low:high])
            return carry

        lax.fori_loop(0, SIDE, add_pair, 0)
        open_stage(part, 2)

    def accumulate(part, stage, value, low, high, others, base):
        index = (c,) + spot(part, stage, value) + (slice(low, high),)
        if stage < 2:
            tail = (slice(None),) * (stage + 1) + (slice(low - base, high - base),)
            plus(index, *[o[tail] for o in others])
        else:
            free = [i for i, s in enumerate(index[:-2]) if isinstance(s, slice)][0]

            def step(i, carry):
                inner = tuple(i if k == free else s for k, s in enumerate(index))
                plus(inner, *[o[i, :, :, low - base : high - base] for o in others])
                return carry

            lax.fori_loop(0, SIDE, step, 0)

    for stage in (2, 1, 0):
        for part in range(3):
            axis = ORDERS[part][stage]
            low, cut, high = rs_parts[part]
            after, before = shifted(axis, 1)[axis], shifted(axis, SIDE - 1)[axis]
            k = part * 3 + stage
            copy_of(part, stage, 0).wait_recv()
            accumulate(part, stage, after, low, cut, [fa[k]], low)
            go(copy_of(part, stage, 4))
            copy_of(part, stage, 1).wait_recv()
            accumulate(part, stage, before, cut, high, [fb[k]], cut)
            go(copy_of(part, stage, 5))
        for part in range(3):
            axis = ORDERS[part][stage]
            low, cut, high = rs_parts[part]
            k = part * 3 + stage
            for kind in range(2, 6):
                copy_of(part, stage, kind).wait_recv()
            accumulate(part, stage, me[axis], low, high, [rl[k], rr[k]], low)
            if stage:
                open_stage(part, stage - 1)

    back = remote(ps.at[(c,) + me], fin, ex_s, ex_r, twin)
    back.start()
    out[c] = ps[(c,) + me]
    back.wait()
    out[other] = fin[...]
    for copy in sent:
        copy.wait_send()


def body(tokens, expert_ids, gate_weights, w_gate, w_up, w_down):
    row_count, model_width = tokens.shape
    half = model_width // 2
    experts, _, hidden_width = w_gate.shape
    c = lax.axis_index("sect")
    catalog = jnp.arange(32, dtype=jnp.int32)
    naming = expert_ids[:, :, None] == catalog[None, None, :]
    share = jnp.sum(jnp.where(naming, gate_weights[:, :, None], 0.0), axis=1)
    high = lax.reduce_precision(share, 8, 7)
    middle = lax.reduce_precision(share - high, 8, 7)
    low = share - high - middle
    extra = jnp.concatenate([high, middle, low, jnp.zeros_like(low)], axis=1).astype(jnp.bfloat16)
    mine = jnp.stack([jnp.concatenate([tokens[:, h * half : (h + 1) * half], extra], axis=1) for h in range(2)])
    spread = jnp.concatenate([mine, mine], axis=1)
    owner = lax.broadcasted_iota(jnp.int32, spread.shape, 1) // row_count
    t8 = jnp.where(owner == c, spread, jnp.zeros_like(spread))

    wide = half + LANES
    sides = (SIDE,) * 3
    bf16 = jnp.bfloat16
    rs_parts = thirds(half)
    lead = [(SIDE,) * s + (8,) for s in range(3)]
    sizes = {
        "fa": [lead[s] + (cut - lo,) for lo, cut, hi in rs_parts for s in range(3)],
        "fb": [lead[s] + (hi - cut,) for lo, cut, hi in rs_parts for s in range(3)],
        "rl": [lead[s] + (hi - lo,) for lo, cut, hi in rs_parts for s in range(3)],
    }
    scratch = [
        pltpu.VMEM((8, wide), bf16),
        pltpu.VMEM((2,) + sides + (8, wide), bf16),
        pltpu.VMEM((model_width, 2 * experts * hidden_width), bf16),
        pltpu.VMEM((2, experts * hidden_width, half), bf16),
        pltpu.VMEM((8 * SIDE**3, experts * hidden_width), bf16),
        pltpu.VMEM((2,) + sides + (8, half), bf16),
        pltpu.VMEM(sides + (8, half), bf16),
    ]
    scratch += [pltpu.VMEM(s, bf16) for key in ("fa", "fb", "rl", "rl") for s in sizes[key]]
    scratch += [pltpu.VMEM((8, half), bf16)]
    dma = pltpu.SemaphoreType.DMA
    scratch += [
        dma((4 * experts,)),
        dma,
        dma,
        dma((3, 3, 4)),
        dma((3, 3, 4)),
        dma((3, 3, 4)),
        dma((3, 3, 4)),
        dma((3,)),
        dma((3,)),
        dma((3, 3, 6)),
        dma((3, 3, 6)),
    ]
    anywhere = pl.BlockSpec(memory_space=pl.ANY)
    vmem = pl.BlockSpec(memory_space=pltpu.VMEM)
    out = pl.pallas_call(
        functools.partial(kernel, half),
        out_shape=jax.ShapeDtypeStruct((2, 8, half), bf16),
        in_specs=[vmem, anywhere, anywhere, anywhere],
        out_specs=vmem,
        scratch_shapes=scratch,
        compiler_params=pltpu.CompilerParams(
            collective_id=0, has_side_effects=True, vmem_limit_bytes=60 * 1024 * 1024
        ),
    )(t8, w_gate, w_up, w_down)
    picked = lax.dynamic_slice_in_dim(out, c * row_count, row_count, axis=1)
    return jnp.concatenate([picked[0], picked[1]], axis=1)


def solution(mesh):
    in_specs = (
        P(ALL, None),
        P(ALL, None),
        P(ALL, None),
        P(("sect", "grp"), None, "dev"),
        P(("sect", "grp"), None, "dev"),
        P(("sect", "grp"), "dev", None),
    )
    return jax.shard_map(body, mesh=mesh, in_specs=in_specs, out_specs=P(ALL, None), check_vma=False)
```

```python
import functools

import jax
import jax.numpy as jnp
from jax import lax
from jax.experimental import pallas as pl
from jax.experimental.pallas import tpu as pltpu
from jax.sharding import PartitionSpec as P

ALL = ("sect", "grp", "dev")
MESH = pl.DeviceIdType.MESH
SIDE = 4
LANES = 128
ORDERS = ((0, 1, 2), (1, 2, 0), (2, 0, 1))


def thirds(width):
    tiles = width // LANES
    counts = [tiles // 3 + (1 if i < tiles % 3 else 0) for i in range(3)]
    parts, low = [], 0
    for count in counts:
        cut = low + (count + 1) // 2 * LANES
        high = low + count * LANES
        parts.append((low, cut, high))
        low = high
    return parts


def kernel(half, t8, wg_hbm, wu_hbm, wd_hbm, out, tr, xs, wall, wd, acc, hid, ps, r0, *rest):
    fa, fb, rl, rr, s1, s0 = (rest[i : i + 3] for i in range(0, 18, 3))
    fin = rest[18]
    wsem, ex_s, ex_r, ag_s, ag_r, dd_s, dd_r, pr_s, pr_r, rs_s, rs_r = rest[19:]
    wide = half + LANES
    experts = wg_hbm.shape[0]
    hidden_width = wg_hbm.shape[2]
    c, g, d = lax.axis_index("sect"), lax.axis_index("grp"), lax.axis_index("dev")
    other = 1 - c
    me = (g // 2, d % SIDE, (g % 2) * 2 + d // SIDE)

    def device(pos, core):
        x, y, z = pos
        return {"sect": core, "grp": x * 2 + z // 2, "dev": (z % 2) * SIDE + y}

    def shifted(axis, by):
        return tuple(lax.rem(m + by, SIDE) if a == axis else m for a, m in enumerate(me))

    twin = device(me, other)
    right = [device(shifted(a, 1), c) for a in range(3)]
    left = [device(shifted(a, SIDE - 1), c) for a in range(3)]
    far = [device(shifted(a, 2), c) for a in range(3)]
    toward = {1: right, 2: far, 3: left}

    barrier = pltpu.get_barrier_semaphore()
    for peer in [twin] + right + left + far:
        pl.semaphore_signal(barrier, inc=1, device_id=peer, device_id_type=MESH)

    weights = []
    for j in range(experts):
        for i, src in enumerate((wg_hbm, wu_hbm)):
            at = (2 * j + i) * hidden_width
            for h in range(2):
              weights.append(
                pltpu.make_async_copy(src.at[j, h * half : (h + 1) * half], wall.at[h, :, at : at + hidden_width], wsem.at[h, 2 * j + i])
            )
    for j in range(experts):
        for h in range(2):
            weights.append(
                pltpu.make_async_copy(
                    wd_hbm.at[j, :, h * half : (h + 1) * half],
                    wd.at[h, j * hidden_width : (j + 1) * hidden_width],
                    wsem.at[h, 2 * experts + j],
                )
            )
    for copy in weights:
        copy.start()
    pl.semaphore_wait(barrier, 10)

    def remote(src, dst, send, recv, peer):
        return pltpu.make_async_remote_copy(
            src_ref=src, dst_ref=dst, send_sem=send, recv_sem=recv, device_id=peer, device_id_type=MESH
        )

    def spot(part, stage, value):
        order = ORDERS[part]
        index = []
        for axis in range(3):
            if axis in order[:stage]:
                index.append(slice(None))
            elif axis == order[stage]:
                index.append(value)
            else:
                index.append(me[axis])
        return tuple(index) + (slice(None),)

    sent = []

    def go(copy):
        copy.start()
        sent.append(copy)

    swap = remote(t8.at[other], tr, ex_s, ex_r, twin)
    swap.start()
    swap.wait()
    xs[(c,) + me] = t8[c] + tr[...]

    ag_parts = thirds(wide)
    steps = (1, SIDE - 1, 2)

    def block(core_half, part, stage, value):
        low, _, high = ag_parts[part]
        return xs.at[(core_half,) + spot(part, stage, value) + (slice(low, high),)]

    def line(core_half, part, second, third):
        low, _, high = ag_parts[part]
        index = [slice(None)] * 3
        index[ORDERS[part][1]] = second
        index[ORDERS[part][2]] = third
        return xs.at[(core_half,) + tuple(index) + (slice(None), slice(low, high))]

    def coord(part, stage, by):
        axis = ORDERS[part][stage]
        return shifted(axis, by)[axis]

    def ag(part, slot, ref, peer):
        return remote(ref, ref, ag_s.at[part, slot], ag_r.at[part, slot], peer)

    def across(part, slot, ref):
        return remote(ref, ref, dd_s.at[part, slot], dd_r.at[part, slot], twin)

    def send_line(part, row, second):
        ref = line(c, part, second, coord(part, 2, 0))
        for k, by in enumerate(steps):
            go(ag(part, 6 + 4 * k + row, ref, toward[by][ORDERS[part][2]]))
        go(across(part, row, ref))

    for part in range(3):
        ref = block(c, part, 0, coord(part, 0, 0))
        for k, by in enumerate(steps):
            go(ag(part, k, ref, toward[by][ORDERS[part][0]]))
    acc[...] = jnp.zeros_like(acc)
    for part in range(3):
        for k, by in enumerate(steps):
            ag(part, k, block(c, part, 0, coord(part, 0, SIDE - by)), twin).wait_recv()
        ref = line(c, part, coord(part, 1, 0), coord(part, 2, 0))
        for k, by in enumerate(steps):
            go(ag(part, 3 + k, ref, toward[by][ORDERS[part][1]]))
        send_line(part, 0, coord(part, 1, 0))
    for k, by in enumerate(steps):
        for part in range(3):
            second = coord(part, 1, SIDE - by)
            ag(part, 3 + k, line(c, part, second, coord(part, 2, 0)), twin).wait_recv()
            send_line(part, 1 + k, second)

    def piece(core_half, part, third):
        low, _, high = ag_parts[part]
        high = min(high, half)
        at = spot(part, 2, third)
        value = xs[(core_half,) + at + (slice(low, high),)].reshape(SIDE * SIDE * 8, high - low)
        got = jnp.dot(value, wall[core_half, low:high, :], preferred_element_type=jnp.float32)
        acc[at + (slice(None),)] += got.reshape(SIDE, SIDE, 8, acc.shape[-1])

    for copy in weights:
        copy.wait()
    for part in range(3):
        piece(c, part, coord(part, 2, 0))
    for part in range(3):
        for row, by in enumerate((0,) + steps):
            across(part, row, line(other, part, coord(part, 1, SIDE - by), coord(part, 2, 0))).wait_recv()
        piece(other, part, coord(part, 2, 0))
    for k, by in enumerate(steps):
        for part in range(3):
            third = coord(part, 2, SIDE - by)
            for row, back_by in enumerate((0,) + steps):
                ag(part, 6 + 4 * k + row, line(c, part, coord(part, 1, SIDE - back_by), third), twin).wait_recv()
            go(across(part, 4 + k, block(c, part, 2, third)))
            piece(c, part, third)
        for part in range(3):
            third = coord(part, 2, SIDE - by)
            across(part, 4 + k, block(other, part, 2, third)).wait_recv()
            piece(other, part, third)

    first = (c * 8 + g) * experts
    row = lax.broadcasted_iota(jnp.int32, (LANES, hidden_width), 0)
    picks = []
    for j in range(experts):
        e = first + j
        hit = (row == e) | (row == e + 32) | (row == e + 64)
        picks.append(jnp.where(hit, 1.0, 0.0).astype(jnp.bfloat16))
    slab = SIDE * SIDE * 8

    def act_step(i, carry):
        share = xs[0, i, :, :, :, half:wide].reshape(slab, LANES)
        for j in range(experts):
            at = 2 * j * hidden_width
            gate = acc[i, :, :, :, at : at + hidden_width].reshape(slab, hidden_width)
            up = acc[i, :, :, :, at + hidden_width : at + 2 * hidden_width].reshape(slab, hidden_width)
            weight = jnp.dot(share, picks[j], preferred_element_type=jnp.float32)
            act = gate / (1.0 + jnp.exp(-gate)) * up * weight
            hid[pl.ds(pl.multiple_of(i * slab, slab), slab), j * hidden_width : (j + 1) * hidden_width] = act.astype(
                jnp.bfloat16
            )
        return carry

    lax.fori_loop(0, SIDE, act_step, 0)
    span = 2
    rows = span * slab

    rs_parts = thirds(half)

    def bounds(part, sub):
        low, cut, high = rs_parts[part]
        return (low, cut) if sub == 0 else (cut, high)

    def down(half_index, part, sub):
        low, high = bounds(part, sub)

        def step(m, carry):
            value = jnp.dot(
                hid[pl.ds(pl.multiple_of(m * rows, rows), rows), :],
                wd[half_index, :, low:high],
                preferred_element_type=jnp.float32,
            ).astype(jnp.bfloat16)
            ps[half_index, pl.ds(m * span, span), :, :, :, low:high] = value.reshape(
                span, SIDE, SIDE, 8, high - low
            )
            return carry

        lax.fori_loop(0, SIDE // span, step, 0)

    def pair(half_index, part, sub):
        low, high = bounds(part, sub)
        cols = (slice(None),) * 4 + (slice(low, high),)
        return remote(
            ps.at[(half_index,) + cols], r0.at[cols], pr_s.at[part, sub], pr_r.at[part, sub], twin
        )

    def plus(index, *others):
        total = ps[index].astype(jnp.float32)
        for value in others:
            total += value.astype(jnp.float32)
        ps[index] = total.astype(jnp.bfloat16)

    def add_pair(part, sub):
        low, high = bounds(part, sub)

        def step(i, carry):
            plus((c, i, slice(None), slice(None), slice(None), slice(low, high)), r0[i, :, :, :, low:high])
            return carry

        lax.fori_loop(0, SIDE, step, 0)

    def big(part, kind):
        axis = ORDERS[part][2]
        low, cut, high = rs_parts[part]
        by, start, stop, buf, peer = (
            (2, low, cut, fa, right),
            (2, cut, high, fb, left),
            (1, cut, high, rl, right),
            (SIDE - 1, low, cut, rr, left),
            (1, low, cut, rl, right),
            (SIDE - 1, cut, high, rr, left),
        )[kind]
        ref = ps.at[(c,) + spot(part, 2, shifted(axis, by)[axis]) + (slice(start, stop),)]
        dst = buf[part]
        if kind > 1:
            dst = dst.at[:, :, :, start - low : stop - low]
        return remote(ref, dst, rs_s.at[part, kind], rs_r.at[part, kind], peer[axis])

    def small(part, stage, k):
        axis = ORDERS[part][stage]
        low, _, high = rs_parts[part]
        ref = ps.at[(c,) + spot(part, stage, shifted(axis, steps[k])[axis]) + (slice(low, high),)]
        dst = (s0, s1)[stage][part].at[k]
        return remote(
            ref, dst, rs_s.at[part, 6 + 3 * stage + k], rs_r.at[part, 6 + 3 * stage + k], toward[steps[k]][axis]
        )

    def accumulate(part, by, low, high, others):
        axis = ORDERS[part][2]
        base = rs_parts[part][0]
        index = (c,) + spot(part, 2, shifted(axis, by)[axis]) + (slice(low, high),)
        free = [i for i, s in enumerate(index[:-2]) if isinstance(s, slice)][0]

        def step(i, carry):
            inner = tuple(i if k == free else s for k, s in enumerate(index))
            plus(inner, *[o[i, :, :, at : at + high - low] for o, at in others])
            return carry

        lax.fori_loop(0, SIDE, step, 0)

    queue = [(part, sub) for sub in range(2) for part in range(3)]
    down(other, *queue[0])
    go(pair(other, *queue[0]))
    for i, (part, sub) in enumerate(queue):
        if i + 1 < len(queue):
            down(other, *queue[i + 1])
            go(pair(other, *queue[i + 1]))
        down(c, part, sub)
        pair(c, part, sub).wait_recv()
        add_pair(part, sub)
        for kind in ((0, 3), (1, 2))[sub]:
            go(big(part, kind))
    for part in range(3):
        low, cut, high = rs_parts[part]
        big(part, 0).wait_recv()
        accumulate(part, 1, low, cut, [(fa[part], 0)])
        go(big(part, 4))
    for part in range(3):
        low, cut, high = rs_parts[part]
        big(part, 1).wait_recv()
        accumulate(part, SIDE - 1, cut, high, [(fb[part], 0)])
        go(big(part, 5))
    for part in range(3):
        low, cut, high = rs_parts[part]
        for kind in range(2, 6):
            big(part, kind).wait_recv()
        accumulate(part, 0, low, high, [(rl[part], 0), (rr[part], 0)])
        for k in range(3):
            go(small(part, 1, k))
    for stage in (1, 0):
        for part in range(3):
            low, cut, high = rs_parts[part]
            for k in range(3):
                small(part, stage, k).wait_recv()
            index = (c,) + spot(part, stage, me[ORDERS[part][stage]]) + (slice(low, high),)
            plus(index, *[(s0, s1)[stage][part][k] for k in range(3)])
            if stage:
                for k in range(3):
                    go(small(part, 0, k))

    back = remote(ps.at[(c,) + me], fin, ex_s, ex_r, twin)
    back.start()
    out[c] = ps[(c,) + me]
    back.wait()
    out[other] = fin[...]
    for copy in sent:
        copy.wait_send()


def body(tokens, expert_ids, gate_weights, w_gate, w_up, w_down):
    row_count, model_width = tokens.shape
    half = model_width // 2
    experts, _, hidden_width = w_gate.shape
    c = lax.axis_index("sect")
    catalog = jnp.arange(32, dtype=jnp.int32)
    naming = expert_ids[:, :, None] == catalog[None, None, :]
    share = jnp.sum(jnp.where(naming, gate_weights[:, :, None], 0.0), axis=1)
    high = lax.reduce_precision(share, 8, 7)
    middle = lax.reduce_precision(share - high, 8, 7)
    low = share - high - middle
    extra = jnp.concatenate([high, middle, low, jnp.zeros_like(low)], axis=1).astype(jnp.bfloat16)
    mine = jnp.stack([jnp.concatenate([tokens[:, h * half : (h + 1) * half], extra], axis=1) for h in range(2)])
    spread = jnp.concatenate([mine, mine], axis=1)
    owner = lax.broadcasted_iota(jnp.int32, spread.shape, 1) // row_count
    t8 = jnp.where(owner == c, spread, jnp.zeros_like(spread))

    wide = half + LANES
    sides = (SIDE,) * 3
    bf16 = jnp.bfloat16
    rs_parts = thirds(half)
    plane = (SIDE, SIDE, 8)
    landing = [plane + (cut - lo,) for lo, cut, hi in rs_parts]
    landing += [plane + (hi - cut,) for lo, cut, hi in rs_parts]
    landing += [plane + (hi - lo,) for lo, cut, hi in rs_parts] * 2
    landing += [(3, SIDE, 8, hi - lo) for lo, cut, hi in rs_parts]
    landing += [(3, 8, hi - lo) for lo, cut, hi in rs_parts]
    scratch = [
        pltpu.VMEM((8, wide), bf16),
        pltpu.VMEM((2,) + sides + (8, wide), bf16),
        pltpu.VMEM((2, half, 2 * experts * hidden_width), bf16),
        pltpu.VMEM((2, experts * hidden_width, half), bf16),
        pltpu.VMEM(sides + (8, 2 * experts * hidden_width), jnp.float32),
        pltpu.VMEM((8 * SIDE**3, experts * hidden_width), bf16),
        pltpu.VMEM((2,) + sides + (8, half), bf16),
        pltpu.VMEM(sides + (8, half), bf16),
    ]
    scratch += [pltpu.VMEM(s, bf16) for s in landing]
    scratch += [pltpu.VMEM((8, half), bf16)]
    dma = pltpu.SemaphoreType.DMA
    scratch += [
        dma((2, 3 * experts)),
        dma,
        dma,
        dma((3, 18)),
        dma((3, 18)),
        dma((3, 7)),
        dma((3, 7)),
        dma((3, 2)),
        dma((3, 2)),
        dma((3, 12)),
        dma((3, 12)),
    ]
    anywhere = pl.BlockSpec(memory_space=pl.ANY)
    vmem = pl.BlockSpec(memory_space=pltpu.VMEM)
    out = pl.pallas_call(
        functools.partial(kernel, half),
        out_shape=jax.ShapeDtypeStruct((2, 8, half), bf16),
        in_specs=[vmem, anywhere, anywhere, anywhere],
        out_specs=vmem,
        scratch_shapes=scratch,
        compiler_params=pltpu.CompilerParams(
            collective_id=0, has_side_effects=True, vmem_limit_bytes=60 * 1024 * 1024
        ),
    )(t8, w_gate, w_up, w_down)
    picked = lax.dynamic_slice_in_dim(out, c * row_count, row_count, axis=1)
    return jnp.concatenate([picked[0], picked[1]], axis=1)


def solution(mesh):
    in_specs = (
        P(ALL, None),
        P(ALL, None),
        P(ALL, None),
        P(("sect", "grp"), None, "dev"),
        P(("sect", "grp"), None, "dev"),
        P(("sect", "grp"), "dev", None),
    )
    return jax.shard_map(body, mesh=mesh, in_specs=in_specs, out_specs=P(ALL, None), check_vma=False)
```

```python
import functools

import jax
import jax.numpy as jnp
from jax import lax
from jax.experimental import pallas as pl
from jax.experimental.pallas import tpu as pltpu
from jax.sharding import PartitionSpec as P

ALL = ("sect", "grp", "dev")
MESH = pl.DeviceIdType.MESH
SIDE = 4
LANES = 128
TILE = 256
ORDERS = ((0, 1, 2), (1, 2, 0), (2, 0, 1)) * 2


GATHER = (6, 6, 4, 4, 4, 5)
SCATTER = (6, 6, 4, 4, 4, 4)


def split(counts):
    parts, low = [], 0
    for count in counts:
        cut = low + (count + 1) // 2 * LANES
        high = low + count * LANES
        parts.append((low, cut, high))
        low = high
    return parts


def kernel(half, tokens, ids, shares, wg_hbm, wu_hbm, wd_hbm, out, t8, tr, xs, wall, wd, acc, hid, ps, r0, *rest):
    fa, fb, rl, rr, s1, s0 = (rest[i : i + 6] for i in range(0, 36, 6))
    fin = rest[36]
    wsem, ex_s, ex_r, ag_s, ag_r, dd_s, dd_r, pr_s, pr_r, rs_s, rs_r = rest[37:]
    wide = half + LANES
    experts = wg_hbm.shape[0]
    hidden_width = wg_hbm.shape[2]
    c, g, d = lax.axis_index("sect"), lax.axis_index("grp"), lax.axis_index("dev")
    other = 1 - c
    me = (g // 2, d % SIDE, (g % 2) * 2 + d // SIDE)

    def device(pos, core):
        x, y, z = pos
        return {"sect": core, "grp": x * 2 + z // 2, "dev": (z % 2) * SIDE + y}

    def shifted(axis, by):
        return tuple(lax.rem(m + by, SIDE) if a == axis else m for a, m in enumerate(me))

    twin = device(me, other)
    right = [device(shifted(a, 1), c) for a in range(3)]
    left = [device(shifted(a, SIDE - 1), c) for a in range(3)]
    far = [device(shifted(a, 2), c) for a in range(3)]
    toward = {1: right, 2: far, 3: left}

    barrier = pltpu.get_barrier_semaphore()
    for peer in [twin] + right + left + far:
        pl.semaphore_signal(barrier, inc=1, device_id=peer, device_id_type=MESH)

    weights = []
    for j in range(experts):
        for i, src in enumerate((wg_hbm, wu_hbm)):
            at = (2 * j + i) * hidden_width
            for h in range(2):
              weights.append(
                pltpu.make_async_copy(src.at[j, h * half : (h + 1) * half], wall.at[h, :, at : at + hidden_width], wsem.at[h, 2 * j + i])
            )
    for j in range(experts):
        for h in range(2):
            weights.append(
                pltpu.make_async_copy(
                    wd_hbm.at[j, :, h * half : (h + 1) * half],
                    wd.at[h, j * hidden_width : (j + 1) * hidden_width],
                    wsem.at[h, 2 * experts + j],
                )
            )
    for copy in weights:
        copy.start()
    lane = lax.broadcasted_iota(jnp.int32, (4, LANES), 1)
    share = jnp.zeros((4, LANES), jnp.float32)
    for k in range(ids.shape[1]):
        share += jnp.where((lane & 31) == ids[:, k : k + 1], shares[:, k : k + 1], 0.0)
    upper = share.astype(jnp.bfloat16).astype(jnp.float32)
    middle = (share - upper).astype(jnp.bfloat16).astype(jnp.float32)
    lower = share - upper - middle
    extra = jnp.where(lane < 32, upper, jnp.where(lane < 64, middle, jnp.where(lane < 96, lower, 0.0)))
    for h in range(2):
        for low, high, value in (
            (0, half, tokens[:, h * half : (h + 1) * half].astype(jnp.float32)),
            (half, wide, extra),
        ):
            eight = jnp.concatenate([value, value], axis=0)
            owner = lax.broadcasted_iota(jnp.int32, eight.shape, 0) // 4
            t8[h, :, low:high] = jnp.where(owner == c, eight, 0.0).astype(jnp.bfloat16)
    pl.semaphore_wait(barrier, 10)

    def remote(src, dst, send, recv, peer):
        return pltpu.make_async_remote_copy(
            src_ref=src, dst_ref=dst, send_sem=send, recv_sem=recv, device_id=peer, device_id_type=MESH
        )

    def spot(part, stage, value):
        order = ORDERS[part]
        index = []
        for axis in range(3):
            if axis in order[:stage]:
                index.append(slice(None))
            elif axis == order[stage]:
                index.append(value)
            else:
                index.append(me[axis])
        return tuple(index) + (slice(None),)

    sent = []

    def go(copy):
        copy.start()
        sent.append(copy)

    swap = remote(t8.at[other], tr, ex_s, ex_r, twin)
    swap.start()
    swap.wait()
    xs[(c,) + me] = t8[c] + tr[...]

    slab = SIDE * SIDE * 8
    ag_parts = split(GATHER)
    steps = (1, SIDE - 1, 2)

    def block(core_half, part, stage, value):
        low, _, high = ag_parts[part]
        return xs.at[(core_half,) + spot(part, stage, value) + (slice(low, high),)]

    def line(core_half, part, second, third):
        low, _, high = ag_parts[part]
        index = [slice(None)] * 3
        index[ORDERS[part][1]] = second
        index[ORDERS[part][2]] = third
        return xs.at[(core_half,) + tuple(index) + (slice(None), slice(low, high))]

    def coord(part, stage, by):
        axis = ORDERS[part][stage]
        return shifted(axis, by)[axis]

    def ag(part, slot, ref, peer):
        return remote(ref, ref, ag_s.at[part, slot], ag_r.at[part, slot], peer)

    def across(part, slot, ref):
        return remote(ref, ref, dd_s.at[part, slot], dd_r.at[part, slot], twin)

    def halved(part, sub, third):
        low, cut, high = ag_parts[part]
        cols = slice(low, cut) if sub == 0 else slice(cut, high)
        return xs.at[(c,) + spot(part, 2, third) + (cols,)]

    def pieces(core_half, part, *thirds):
        low, _, high = ag_parts[part]
        high = min(high, half)
        spots = [spot(part, 2, third) for third in thirds]
        values = [xs[(core_half,) + at + (slice(low, high),)].reshape(slab, high - low) for at in spots]
        value = values[0] if len(values) == 1 else jnp.concatenate(values, axis=0)
        for start in range(0, acc.shape[-1], TILE):
            got = jnp.dot(value, wall[core_half, low:high, start : start + TILE], preferred_element_type=jnp.float32)
            for i, at in enumerate(spots):
                mine = got[i * slab : (i + 1) * slab].reshape(SIDE, SIDE, 8, TILE)
                acc[at + (slice(start, start + TILE),)] += mine

    def first_hop(part):
        ref = block(c, part, 0, coord(part, 0, 0))
        for k, by in enumerate(steps):
            go(ag(part, k, ref, toward[by][ORDERS[part][0]]))

    def second_hop(part):
        for k, by in enumerate(steps):
            ag(part, k, block(c, part, 0, coord(part, 0, SIDE - by)), twin).wait_recv()
        ref = line(c, part, coord(part, 1, 0), coord(part, 2, 0))
        for k, by in enumerate(steps):
            go(ag(part, 3 + k, ref, toward[by][ORDERS[part][1]]))

    def third_hop(part, row):
        by = (0,) + steps
        ref = line(c, part, coord(part, 1, SIDE - by[row]), coord(part, 2, 0))
        if row:
            ag(part, 2 + row, ref, twin).wait_recv()
        go(ag(part, 6 + row, ref, right[ORDERS[part][2]]))
        go(ag(part, 10 + row, ref, left[ORDERS[part][2]]))
        if row == 3:
            go(across(part, 0, block(c, part, 2, coord(part, 2, 0))))

    def fourth_hop(part):
        axis = ORDERS[part][2]
        before, after = coord(part, 2, SIDE - 1), coord(part, 2, 1)
        for third, slot, sub, peer in ((before, 6, 0, right[axis]), (after, 10, 1, left[axis])):
            for row, by in enumerate((0,) + steps):
                ag(part, slot + row, line(c, part, coord(part, 1, SIDE - by), third), twin).wait_recv()
            go(ag(part, 14 + sub, halved(part, sub, third), peer))
        go(across(part, 1, block(c, part, 2, before)))
        go(across(part, 2, block(c, part, 2, after)))

    def last_hop(part):
        opposite = coord(part, 2, 2)
        ag(part, 14, halved(part, 0, opposite), twin).wait_recv()
        ag(part, 15, halved(part, 1, opposite), twin).wait_recv()
        go(across(part, 3, block(c, part, 2, opposite)))

    def arrived(part, slot):
        value = coord(part, 2, (0, SIDE - 1, 1, 2)[slot])
        across(part, slot, block(other, part, 2, value)).wait_recv()

    early, late = range(3), range(3, 6)
    for part in range(6):
        first_hop(part)
    acc[...] = jnp.zeros_like(acc)
    for wave in (early, late):
        for part in wave:
            second_hop(part)
        for part in wave:
            third_hop(part, 0)
    for wave in (early, late):
        for row in range(1, SIDE):
            for part in wave:
                third_hop(part, row)
    for copy in weights:
        copy.wait()
    for wave in (early, late):
        for part in wave:
            pieces(c, part, coord(part, 2, 0))
    for part in early:
        fourth_hop(part)
    for wave in (early, late):
        for part in wave:
            arrived(part, 0)
            pieces(other, part, coord(part, 2, 0))
    for part in late:
        fourth_hop(part)
    for wave in (early, late):
        for part in wave:
            pieces(c, part, coord(part, 2, 1), coord(part, 2, SIDE - 1))
    for part in early:
        last_hop(part)
    for wave in (early, late):
        for part in wave:
            arrived(part, 1)
            arrived(part, 2)
            pieces(other, part, coord(part, 2, 1), coord(part, 2, SIDE - 1))
    for part in late:
        last_hop(part)
    for wave in (early, late):
        for part in wave:
            pieces(c, part, coord(part, 2, 2))
    for wave in (early, late):
        for part in wave:
            arrived(part, 3)
            pieces(other, part, coord(part, 2, 2))

    first = (c * 8 + g) * experts
    row = lax.broadcasted_iota(jnp.int32, (LANES, hidden_width), 0)
    picks = []
    for j in range(experts):
        e = first + j
        hit = (row == e) | (row == e + 32) | (row == e + 64)
        picks.append(jnp.where(hit, 1.0, 0.0).astype(jnp.bfloat16))
    def act_step(i, carry):
        share = xs[0, i, :, :, :, half:wide].reshape(slab, LANES)
        for j in range(experts):
            at = 2 * j * hidden_width
            gate = acc[i, :, :, :, at : at + hidden_width].reshape(slab, hidden_width)
            up = acc[i, :, :, :, at + hidden_width : at + 2 * hidden_width].reshape(slab, hidden_width)
            weight = jnp.dot(share, picks[j], preferred_element_type=jnp.float32)
            act = gate / (1.0 + jnp.exp(-gate)) * up * weight
            hid[pl.ds(pl.multiple_of(i * slab, slab), slab), j * hidden_width : (j + 1) * hidden_width] = act.astype(
                jnp.bfloat16
            )
        return carry

    lax.fori_loop(0, SIDE, act_step, 0)

    rs_parts = split(SCATTER)

    def down(half_index, part, add):
        low, _, high = rs_parts[part]

        value = hid[...]
        for start in range(low, high, TILE):
            stop = min(start + TILE, high)
            at = (slice(None),) * 4 + (slice(start, stop),)
            got = jnp.dot(value, wd[half_index, :, start:stop], preferred_element_type=jnp.float32)
            if add:
                got += r0[at].reshape(got.shape).astype(jnp.float32)
            ps[(half_index,) + at] = got.astype(jnp.bfloat16).reshape(SIDE, SIDE, SIDE, 8, stop - start)

    def pair(half_index, part):
        low, _, high = rs_parts[part]
        cols = (slice(None),) * 4 + (slice(low, high),)
        return remote(ps.at[(half_index,) + cols], r0.at[cols], pr_s.at[part], pr_r.at[part], twin)

    def plus(index, *others):
        total = ps[index].astype(jnp.float32)
        for value in others:
            total += value.astype(jnp.float32)
        ps[index] = total.astype(jnp.bfloat16)

    def big(part, kind):
        axis = ORDERS[part][2]
        low, cut, high = rs_parts[part]
        by, start, stop, buf, peer = (
            (2, low, cut, fa, right),
            (2, cut, high, fb, left),
            (1, cut, high, rl, right),
            (SIDE - 1, low, cut, rr, left),
            (1, low, cut, rl, right),
            (SIDE - 1, cut, high, rr, left),
        )[kind]
        ref = ps.at[(c,) + spot(part, 2, shifted(axis, by)[axis]) + (slice(start, stop),)]
        dst = buf[part]
        if kind > 1:
            dst = dst.at[:, :, :, start - low : stop - low]
        return remote(ref, dst, rs_s.at[part, kind], rs_r.at[part, kind], peer[axis])

    def small(part, stage, k):
        axis = ORDERS[part][stage]
        low, _, high = rs_parts[part]
        ref = ps.at[(c,) + spot(part, stage, shifted(axis, steps[k])[axis]) + (slice(low, high),)]
        dst = (s0, s1)[stage][part].at[k]
        return remote(
            ref, dst, rs_s.at[part, 6 + 3 * stage + k], rs_r.at[part, 6 + 3 * stage + k], toward[steps[k]][axis]
        )

    def accumulate(part, by, low, high, others):
        axis = ORDERS[part][2]
        base = rs_parts[part][0]
        index = (c,) + spot(part, 2, shifted(axis, by)[axis]) + (slice(low, high),)
        free = [i for i, s in enumerate(index[:-2]) if isinstance(s, slice)][0]

        def step(i, carry):
            inner = tuple(i if k == free else s for k, s in enumerate(index))
            plus(inner, *[o[i, :, :, at : at + high - low] for o, at in others])
            return carry

        lax.fori_loop(0, SIDE, step, 0)

    def forward(part):
        low, cut, high = rs_parts[part]
        big(part, 0).wait_recv()
        accumulate(part, 1, low, cut, [(fa[part], 0)])
        go(big(part, 4))
        big(part, 1).wait_recv()
        accumulate(part, SIDE - 1, cut, high, [(fb[part], 0)])
        go(big(part, 5))

    def settle(part):
        low, cut, high = rs_parts[part]
        for kind in range(2, 6):
            big(part, kind).wait_recv()
        accumulate(part, 0, low, high, [(rl[part], 0), (rr[part], 0)])
        for k in range(3):
            go(small(part, 1, k))

    def finish_axis(part, stage):
        low, cut, high = rs_parts[part]
        for k in range(3):
            small(part, stage, k).wait_recv()
        index = (c,) + spot(part, stage, me[ORDERS[part][stage]]) + (slice(low, high),)
        plus(index, *[(s0, s1)[stage][part][k] for k in range(3)])
        if stage:
            for k in range(3):
                go(small(part, 0, k))

    ahead = 3
    for part in range(ahead):
        down(other, part, False)
        go(pair(other, part))
    for part in range(6):
        if part + ahead < 6:
            down(other, part + ahead, False)
            go(pair(other, part + ahead))
        pair(c, part).wait_recv()
        down(c, part, True)
        for kind in range(4):
            go(big(part, kind))
        if part >= 3:
            forward(part - 3)
    for part in late:
        forward(part)
    for part in range(6):
        settle(part)
    for stage in (1, 0):
        for part in range(6):
            finish_axis(part, stage)

    back = remote(ps.at[(c,) + me], fin, ex_s, ex_r, twin)
    back.start()
    out[:, pl.ds(pl.multiple_of(c * half, half), half)] = ps[(c,) + me]
    back.wait()
    out[:, pl.ds(pl.multiple_of(other * half, half), half)] = fin[...]
    for copy in sent:
        copy.wait_send()


def body(tokens, expert_ids, gate_weights, w_gate, w_up, w_down):
    row_count, model_width = tokens.shape
    half = model_width // 2
    experts, _, hidden_width = w_gate.shape
    c = lax.axis_index("sect")
    wide = half + LANES
    sides = (SIDE,) * 3
    bf16 = jnp.bfloat16
    rs_parts = split(SCATTER)
    plane = (SIDE, SIDE, 8)
    landing = [plane + (cut - lo,) for lo, cut, hi in rs_parts]
    landing += [plane + (hi - cut,) for lo, cut, hi in rs_parts]
    landing += [plane + (hi - lo,) for lo, cut, hi in rs_parts] * 2
    landing += [(3, SIDE, 8, hi - lo) for lo, cut, hi in rs_parts]
    landing += [(3, 8, hi - lo) for lo, cut, hi in rs_parts]
    scratch = [
        pltpu.VMEM((2, 8, wide), bf16),
        pltpu.VMEM((8, wide), bf16),
        pltpu.VMEM((2,) + sides + (8, wide), bf16),
        pltpu.VMEM((2, half, 2 * experts * hidden_width), bf16),
        pltpu.VMEM((2, experts * hidden_width, half), bf16),
        pltpu.VMEM(sides + (8, 2 * experts * hidden_width), jnp.float32),
        pltpu.VMEM((8 * SIDE**3, experts * hidden_width), bf16),
        pltpu.VMEM((2,) + sides + (8, half), bf16),
        pltpu.VMEM(sides + (8, half), bf16),
    ]
    scratch += [pltpu.VMEM(s, bf16) for s in landing]
    scratch += [pltpu.VMEM((8, half), bf16)]
    dma = pltpu.SemaphoreType.DMA
    scratch += [
        dma((2, 3 * experts)),
        dma,
        dma,
        dma((6, 16)),
        dma((6, 16)),
        dma((6, 4)),
        dma((6, 4)),
        dma((6,)),
        dma((6,)),
        dma((6, 12)),
        dma((6, 12)),
    ]
    anywhere = pl.BlockSpec(memory_space=pl.ANY)
    vmem = pl.BlockSpec(memory_space=pltpu.VMEM)
    out = pl.pallas_call(
        functools.partial(kernel, half),
        out_shape=jax.ShapeDtypeStruct((8, model_width), bf16),
        in_specs=[vmem, vmem, vmem, anywhere, anywhere, anywhere],
        out_specs=vmem,
        scratch_shapes=scratch,
        compiler_params=pltpu.CompilerParams(
            collective_id=0, has_side_effects=True, vmem_limit_bytes=60 * 1024 * 1024
        ),
    )(tokens, expert_ids, gate_weights, w_gate, w_up, w_down)
    return lax.dynamic_slice_in_dim(out, c * row_count, row_count, axis=0)


def solution(mesh):
    in_specs = (
        P(ALL, None),
        P(ALL, None),
        P(ALL, None),
        P(("sect", "grp"), None, "dev"),
        P(("sect", "grp"), None, "dev"),
        P(("sect", "grp"), "dev", None),
    )
    return jax.shard_map(body, mesh=mesh, in_specs=in_specs, out_specs=P(ALL, None), check_vma=False)
```

```python
import functools

import jax
import jax.numpy as jnp
from jax import lax
from jax.experimental import pallas as pl
from jax.experimental.pallas import tpu as pltpu
from jax.sharding import PartitionSpec as P

ALL = ("sect", "grp", "dev")
MESH = pl.DeviceIdType.MESH
SIDE = 4
LANES = 128
TILE = 256
ORDERS = ((0, 1, 2), (1, 2, 0), (2, 0, 1)) * 3
WAVES = (range(0, 3), range(3, 6), range(0))
PARTS = 6
AHEAD = 3
LAG = 6


GATHER = (6, 6, 6, 4, 4, 3)
SCATTER = (6, 6, 6, 4, 4, 2)


def split(counts):
    parts, low = [], 0
    for count in counts:
        cut = low + (count + 1) // 2 * LANES
        high = low + count * LANES
        parts.append((low, cut, high))
        low = high
    return parts


def kernel(half, tokens, ids, shares, wg_hbm, wu_hbm, wd_hbm, out, t8, tr, xs, wall, wd, acc, hid, ps, r0, *rest):
    fa, fb, rl, rr, s1, s0 = (rest[i : i + PARTS] for i in range(0, 6 * PARTS, PARTS))
    fin = rest[6 * PARTS]
    wsem, ex_s, ex_r, ag_s, ag_r, dd_s, dd_r, pr_s, pr_r, rs_s, rs_r, fin_s, fin_r = rest[6 * PARTS + 1 :]
    wide = half + LANES
    experts = wg_hbm.shape[0]
    hidden_width = wg_hbm.shape[2]
    c, g, d = lax.axis_index("sect"), lax.axis_index("grp"), lax.axis_index("dev")
    other = 1 - c
    me = (g // 2, d % SIDE, (g % 2) * 2 + d // SIDE)

    def device(pos, core):
        x, y, z = pos
        return {"sect": core, "grp": x * 2 + z // 2, "dev": (z % 2) * SIDE + y}

    def shifted(axis, by):
        return tuple(lax.rem(m + by, SIDE) if a == axis else m for a, m in enumerate(me))

    twin = device(me, other)
    right = [device(shifted(a, 1), c) for a in range(3)]
    left = [device(shifted(a, SIDE - 1), c) for a in range(3)]
    far = [device(shifted(a, 2), c) for a in range(3)]
    toward = {1: right, 2: far, 3: left}
    cross = {by: [device(shifted(a, by), other) for a in range(3)] for by in (1, 2, 3)}

    barrier = pltpu.get_barrier_semaphore()
    for peer in [twin] + right + left + far + cross[1] + cross[2] + cross[3]:
        pl.semaphore_signal(barrier, inc=1, device_id=peer, device_id_type=MESH)

    weights = []
    for j in range(experts):
        for i, src in enumerate((wg_hbm, wu_hbm)):
            at = (2 * j + i) * hidden_width
            for h in range(2):
              weights.append(
                pltpu.make_async_copy(src.at[j, h * half : (h + 1) * half], wall.at[h, :, at : at + hidden_width], wsem.at[h, 2 * j + i])
            )
    for j in range(experts):
        for h in range(2):
            weights.append(
                pltpu.make_async_copy(
                    wd_hbm.at[j, :, h * half : (h + 1) * half],
                    wd.at[h, j * hidden_width : (j + 1) * hidden_width],
                    wsem.at[h, 2 * experts + j],
                )
            )
    for copy in weights:
        copy.start()
    lane = lax.broadcasted_iota(jnp.int32, (4, LANES), 1)
    share = jnp.zeros((4, LANES), jnp.float32)
    for k in range(ids.shape[1]):
        share += jnp.where((lane & 31) == ids[:, k : k + 1], shares[:, k : k + 1], 0.0)
    upper = share.astype(jnp.bfloat16).astype(jnp.float32)
    middle = (share - upper).astype(jnp.bfloat16).astype(jnp.float32)
    lower = share - upper - middle
    extra = jnp.where(lane < 32, upper, jnp.where(lane < 64, middle, jnp.where(lane < 96, lower, 0.0)))
    for h in range(2):
        for low, high, value in (
            (0, half, tokens[:, h * half : (h + 1) * half].astype(jnp.float32)),
            (half, wide, extra),
        ):
            eight = jnp.concatenate([value, value], axis=0)
            owner = lax.broadcasted_iota(jnp.int32, eight.shape, 0) // 4
            t8[h, :, low:high] = jnp.where(owner == c, eight, 0.0).astype(jnp.bfloat16)
    pl.semaphore_wait(barrier, 19)

    def remote(src, dst, send, recv, peer):
        return pltpu.make_async_remote_copy(
            src_ref=src, dst_ref=dst, send_sem=send, recv_sem=recv, device_id=peer, device_id_type=MESH
        )

    def spot(part, stage, value):
        order = ORDERS[part]
        index = []
        for axis in range(3):
            if axis in order[:stage]:
                index.append(slice(None))
            elif axis == order[stage]:
                index.append(value)
            else:
                index.append(me[axis])
        return tuple(index) + (slice(None),)

    sent = []

    def go(copy):
        copy.start()
        sent.append(copy)

    swap = remote(t8.at[other], tr, ex_s, ex_r, twin)
    swap.start()
    swap.wait()
    xs[(c,) + me] = t8[c] + tr[...]

    slab = SIDE * SIDE * 8
    ag_parts = split(GATHER)
    steps = (1, SIDE - 1, 2)

    def block(core_half, part, stage, value):
        low, _, high = ag_parts[part]
        return xs.at[(core_half,) + spot(part, stage, value) + (slice(low, high),)]

    def line(core_half, part, second, third):
        low, _, high = ag_parts[part]
        index = [slice(None)] * 3
        index[ORDERS[part][1]] = second
        index[ORDERS[part][2]] = third
        return xs.at[(core_half,) + tuple(index) + (slice(None), slice(low, high))]

    def coord(part, stage, by):
        axis = ORDERS[part][stage]
        return shifted(axis, by)[axis]

    def ag(part, slot, ref, peer):
        return remote(ref, ref, ag_s.at[part, slot], ag_r.at[part, slot], peer)

    def across(part, slot, ref):
        return remote(ref, ref, dd_s.at[part, slot], dd_r.at[part, slot], twin)

    def halved(part, sub, third):
        low, cut, high = ag_parts[part]
        cols = slice(low, cut) if sub == 0 else slice(cut, high)
        return xs.at[(c,) + spot(part, 2, third) + (cols,)]

    def pieces(core_half, part, *thirds):
        low, _, high = ag_parts[part]
        high = min(high, half)
        spots = [spot(part, 2, third) for third in thirds]
        values = [xs[(core_half,) + at + (slice(low, high),)].reshape(slab, high - low) for at in spots]
        value = values[0] if len(values) == 1 else jnp.concatenate(values, axis=0)
        for start in range(0, acc.shape[-1], TILE):
            got = jnp.dot(value, wall[core_half, low:high, start : start + TILE], preferred_element_type=jnp.float32)
            for i, at in enumerate(spots):
                mine = got[i * slab : (i + 1) * slab].reshape(SIDE, SIDE, 8, TILE)
                acc[at + (slice(start, start + TILE),)] += mine

    def first_hop(part):
        ref = block(c, part, 0, coord(part, 0, 0))
        for k, by in enumerate(steps):
            go(ag(part, k, ref, toward[by][ORDERS[part][0]]))

    def second_hop(part):
        for k, by in enumerate(steps):
            ag(part, k, block(c, part, 0, coord(part, 0, SIDE - by)), twin).wait_recv()
        ref = line(c, part, coord(part, 1, 0), coord(part, 2, 0))
        for k, by in enumerate(steps):
            go(ag(part, 3 + k, ref, toward[by][ORDERS[part][1]]))

    def third_hop(part, row):
        by = (0,) + steps
        ref = line(c, part, coord(part, 1, SIDE - by[row]), coord(part, 2, 0))
        if row:
            ag(part, 2 + row, ref, twin).wait_recv()
        go(ag(part, 6 + row, ref, right[ORDERS[part][2]]))
        go(ag(part, 10 + row, ref, left[ORDERS[part][2]]))
        if row == 3:
            go(across(part, 0, block(c, part, 2, coord(part, 2, 0))))

    def fourth_hop(part):
        axis = ORDERS[part][2]
        before, after = coord(part, 2, SIDE - 1), coord(part, 2, 1)
        for third, slot, sub, peer in ((before, 6, 0, right[axis]), (after, 10, 1, left[axis])):
            for row, by in enumerate((0,) + steps):
                ag(part, slot + row, line(c, part, coord(part, 1, SIDE - by), third), twin).wait_recv()
            go(ag(part, 14 + sub, halved(part, sub, third), peer))
        go(across(part, 1, block(c, part, 2, before)))
        go(across(part, 2, block(c, part, 2, after)))

    def last_hop(part):
        opposite = coord(part, 2, 2)
        ag(part, 14, halved(part, 0, opposite), twin).wait_recv()
        ag(part, 15, halved(part, 1, opposite), twin).wait_recv()
        go(across(part, 3, block(c, part, 2, opposite)))

    def arrived(part, slot):
        value = coord(part, 2, (0, SIDE - 1, 1, 2)[slot])
        across(part, slot, block(other, part, 2, value)).wait_recv()

    def near(core_half, wave):
        for part in wave:
            if core_half is other:
                arrived(part, 0)
            pieces(core_half, part, coord(part, 2, 0))

    def beside(core_half, wave):
        for part in wave:
            if core_half is other:
                arrived(part, 1)
                arrived(part, 2)
            pieces(core_half, part, coord(part, 2, 1), coord(part, 2, SIDE - 1))

    def opposite(core_half, wave):
        for part in wave:
            if core_half is other:
                arrived(part, 3)
            pieces(core_half, part, coord(part, 2, 2))

    def each(step, wave):
        for part in wave:
            step(part)

    for wave in WAVES:
        each(first_hop, wave)
    acc[...] = jnp.zeros_like(acc)
    for wave in WAVES:
        each(second_hop, wave)
        for part in wave:
            third_hop(part, 0)
    for wave in WAVES:
        for row in range(1, SIDE):
            for part in wave:
                third_hop(part, row)
    for copy in weights:
        copy.wait()
    w0, w1, w2 = WAVES
    near(c, w0)
    near(c, w1)
    each(fourth_hop, w0)
    near(c, w2)
    near(other, w0)
    near(other, w1)
    each(fourth_hop, w1)
    near(other, w2)
    beside(c, w0)
    each(fourth_hop, w2)
    beside(other, w0)
    each(last_hop, w0)
    beside(c, w1)
    beside(other, w1)
    each(last_hop, w1)
    beside(c, w2)
    opposite(c, w0)
    each(last_hop, w2)
    beside(other, w2)
    opposite(other, w0)
    opposite(c, w1)
    opposite(other, w1)
    opposite(c, w2)
    opposite(other, w2)

    first = (c * 8 + g) * experts
    row = lax.broadcasted_iota(jnp.int32, (LANES, hidden_width), 0)
    picks = []
    for j in range(experts):
        e = first + j
        hit = (row == e) | (row == e + 32) | (row == e + 64)
        picks.append(jnp.where(hit, 1.0, 0.0).astype(jnp.bfloat16))
    def act_step(i, carry):
        share = xs[0, i, :, :, :, half:wide].reshape(slab, LANES)
        for j in range(experts):
            at = 2 * j * hidden_width
            gate = acc[i, :, :, :, at : at + hidden_width].reshape(slab, hidden_width)
            up = acc[i, :, :, :, at + hidden_width : at + 2 * hidden_width].reshape(slab, hidden_width)
            weight = jnp.dot(share, picks[j], preferred_element_type=jnp.float32)
            act = gate / (1.0 + jnp.exp(-gate)) * up * weight
            hid[pl.ds(pl.multiple_of(i * slab, slab), slab), j * hidden_width : (j + 1) * hidden_width] = act.astype(
                jnp.bfloat16
            )
        return carry

    lax.fori_loop(0, SIDE, act_step, 0)

    rs_parts = split(SCATTER)

    def down(half_index, part, add):
        low, _, high = rs_parts[part]

        value = hid[...]
        for start in range(low, high, TILE):
            stop = min(start + TILE, high)
            at = (slice(None),) * 4 + (slice(start, stop),)
            got = jnp.dot(value, wd[half_index, :, start:stop], preferred_element_type=jnp.float32)
            if add:
                got += r0[at].reshape(got.shape).astype(jnp.float32)
            ps[(half_index,) + at] = got.astype(jnp.bfloat16).reshape(SIDE, SIDE, SIDE, 8, stop - start)

    def pair(half_index, part):
        low, _, high = rs_parts[part]
        cols = (slice(None),) * 4 + (slice(low, high),)
        return remote(ps.at[(half_index,) + cols], r0.at[cols], pr_s.at[part], pr_r.at[part], twin)

    def plus(index, *others):
        total = ps[index].astype(jnp.float32)
        for value in others:
            total += value.astype(jnp.float32)
        ps[index] = total.astype(jnp.bfloat16)

    def big(part, kind):
        axis = ORDERS[part][2]
        low, cut, high = rs_parts[part]
        by, start, stop, buf, peer = (
            (2, low, cut, fa, right),
            (2, cut, high, fb, left),
            (1, cut, high, rl, right),
            (SIDE - 1, low, cut, rr, left),
            (1, low, cut, rl, right),
            (SIDE - 1, cut, high, rr, left),
        )[kind]
        ref = ps.at[(c,) + spot(part, 2, shifted(axis, by)[axis]) + (slice(start, stop),)]
        dst = buf[part]
        if kind > 1:
            dst = dst.at[:, :, :, start - low : stop - low]
        return remote(ref, dst, rs_s.at[part, kind], rs_r.at[part, kind], peer[axis])

    def small(part, stage, k):
        axis = ORDERS[part][stage]
        low, _, high = rs_parts[part]
        ref = ps.at[(c,) + spot(part, stage, shifted(axis, steps[k])[axis]) + (slice(low, high),)]
        dst = (s0, s1)[stage][part].at[k]
        return remote(
            ref, dst, rs_s.at[part, 6 + 3 * stage + k], rs_r.at[part, 6 + 3 * stage + k], toward[steps[k]][axis]
        )

    def swapped(part, k):
        axis = ORDERS[part][0]
        low, _, high = rs_parts[part]
        peer = cross[steps[k]][axis] if k < 3 else twin
        by = steps[k] if k < 3 else 0
        ref = ps.at[(c,) + spot(part, 0, shifted(axis, by)[axis]) + (slice(low, high),)]
        return remote(ref, fin.at[k, :, low:high], fin_s.at[part, k], fin_r.at[part, k], peer)

    def accumulate(part, by, low, high, others):
        axis = ORDERS[part][2]
        base = rs_parts[part][0]
        index = (c,) + spot(part, 2, shifted(axis, by)[axis]) + (slice(low, high),)
        free = [i for i, s in enumerate(index[:-2]) if isinstance(s, slice)][0]

        def step(i, carry):
            inner = tuple(i if k == free else s for k, s in enumerate(index))
            plus(inner, *[o[i, :, :, at : at + high - low] for o, at in others])
            return carry

        lax.fori_loop(0, SIDE, step, 0)

    def forward(part):
        low, cut, high = rs_parts[part]
        big(part, 0).wait_recv()
        accumulate(part, 1, low, cut, [(fa[part], 0)])
        go(big(part, 4))
        big(part, 1).wait_recv()
        accumulate(part, SIDE - 1, cut, high, [(fb[part], 0)])
        go(big(part, 5))

    def settle(part):
        low, cut, high = rs_parts[part]
        for kind in range(2, 6):
            big(part, kind).wait_recv()
        accumulate(part, 0, low, high, [(rl[part], 0), (rr[part], 0)])
        for k in range(3):
            go(small(part, 1, k))

    def finish_axis(part, stage):
        low, cut, high = rs_parts[part]
        for k in range(3):
            small(part, stage, k).wait_recv()
        index = (c,) + spot(part, stage, me[ORDERS[part][stage]]) + (slice(low, high),)
        if stage == 0:
            total = ps[index].astype(jnp.float32)
            for k in range(3):
                total += s0[part][k].astype(jnp.float32)
            out[:, pl.ds(pl.multiple_of(c * half + low, LANES), high - low)] = total.astype(jnp.bfloat16)
            total = jnp.zeros((8, high - low), jnp.float32)
            for k in range(4):
                swapped(part, k).wait_recv()
                total += fin[k, :, low:high].astype(jnp.float32)
            out[:, pl.ds(pl.multiple_of(other * half + low, LANES), high - low)] = total.astype(jnp.bfloat16)
            return
        plus(index, *[s1[part][k] for k in range(3)])
        if stage:
            for k in range(3):
                go(small(part, 0, k))
                go(swapped(part, k))
            go(swapped(part, 3))

    for part in range(AHEAD):
        down(other, part, False)
        go(pair(other, part))
    for part in range(PARTS):
        if part + AHEAD < PARTS:
            down(other, part + AHEAD, False)
            go(pair(other, part + AHEAD))
        pair(c, part).wait_recv()
        down(c, part, True)
        for kind in range(4):
            go(big(part, kind))
        if part >= LAG:
            forward(part - LAG)
    for part in range(PARTS - LAG, PARTS):
        forward(part)
    each(settle, w0)
    each(settle, w1)
    for part in w0:
        finish_axis(part, 1)
    each(settle, w2)
    for part in w1:
        finish_axis(part, 1)
    for part in w0:
        finish_axis(part, 0)
    for part in w2:
        finish_axis(part, 1)
    for part in w1:
        finish_axis(part, 0)
    for part in w2:
        finish_axis(part, 0)

    for copy in sent:
        copy.wait_send()


def body(tokens, expert_ids, gate_weights, w_gate, w_up, w_down):
    row_count, model_width = tokens.shape
    half = model_width // 2
    experts, _, hidden_width = w_gate.shape
    c = lax.axis_index("sect")
    wide = half + LANES
    sides = (SIDE,) * 3
    bf16 = jnp.bfloat16
    rs_parts = split(SCATTER)
    plane = (SIDE, SIDE, 8)
    landing = [plane + (cut - lo,) for lo, cut, hi in rs_parts]
    landing += [plane + (hi - cut,) for lo, cut, hi in rs_parts]
    landing += [plane + (hi - lo,) for lo, cut, hi in rs_parts] * 2
    landing += [(3, SIDE, 8, hi - lo) for lo, cut, hi in rs_parts]
    landing += [(3, 8, hi - lo) for lo, cut, hi in rs_parts]
    scratch = [
        pltpu.VMEM((2, 8, wide), bf16),
        pltpu.VMEM((8, wide), bf16),
        pltpu.VMEM((2,) + sides + (8, wide), bf16),
        pltpu.VMEM((2, half, 2 * experts * hidden_width), bf16),
        pltpu.VMEM((2, experts * hidden_width, half), bf16),
        pltpu.VMEM(sides + (8, 2 * experts * hidden_width), jnp.float32),
        pltpu.VMEM((8 * SIDE**3, experts * hidden_width), bf16),
        pltpu.VMEM((2,) + sides + (8, half), bf16),
        pltpu.VMEM(sides + (8, half), bf16),
    ]
    scratch += [pltpu.VMEM(s, bf16) for s in landing]
    scratch += [pltpu.VMEM((4, 8, half), bf16)]
    dma = pltpu.SemaphoreType.DMA
    scratch += [
        dma((2, 3 * experts)),
        dma,
        dma,
        dma((PARTS, 16)),
        dma((PARTS, 16)),
        dma((PARTS, 4)),
        dma((PARTS, 4)),
        dma((PARTS,)),
        dma((PARTS,)),
        dma((PARTS, 12)),
        dma((PARTS, 12)),
        dma((PARTS, 4)),
        dma((PARTS, 4)),
    ]
    anywhere = pl.BlockSpec(memory_space=pl.ANY)
    vmem = pl.BlockSpec(memory_space=pltpu.VMEM)
    out = pl.pallas_call(
        functools.partial(kernel, half),
        out_shape=jax.ShapeDtypeStruct((8, model_width), bf16),
        in_specs=[vmem, vmem, vmem, anywhere, anywhere, anywhere],
        out_specs=vmem,
        scratch_shapes=scratch,
        compiler_params=pltpu.CompilerParams(
            collective_id=0, has_side_effects=True, vmem_limit_bytes=60 * 1024 * 1024
        ),
    )(tokens, expert_ids, gate_weights, w_gate, w_up, w_down)
    return lax.dynamic_slice_in_dim(out, c * row_count, row_count, axis=0)


def solution(mesh):
    in_specs = (
        P(ALL, None),
        P(ALL, None),
        P(ALL, None),
        P(("sect", "grp"), None, "dev"),
        P(("sect", "grp"), None, "dev"),
        P(("sect", "grp"), "dev", None),
    )
    return jax.shard_map(body, mesh=mesh, in_specs=in_specs, out_specs=P(ALL, None), check_vma=False)
```

```python
import functools

import jax
import jax.numpy as jnp
from jax import lax
from jax.experimental import pallas as pl
from jax.experimental.pallas import tpu as pltpu
from jax.sharding import PartitionSpec as P

ALL = ("sect", "grp", "dev")
MESH = pl.DeviceIdType.MESH
SIDE = 4
LANES = 128
TILE = 256
ORDERS = ((0, 1, 2), (1, 2, 0), (2, 0, 1)) * 3
WAVES = (range(0, 3), range(3, 6), range(0))
PARTS = 6
AHEAD = 2
LAG = 6


GATHER = (6, 6, 6, 4, 4, 3)
SCATTER = (6, 6, 6, 4, 4, 2)


def split(counts):
    parts, low = [], 0
    for count in counts:
        cut = low + (count + 1) // 2 * LANES
        high = low + count * LANES
        parts.append((low, cut, high))
        low = high
    return parts


def kernel(half, tokens, ids, shares, wg_hbm, wu_hbm, wd_hbm, out, t8, tr, xs, wall, wd, acc, hid, ps, r0, *rest):
    fa, fb, rl, rr, s1, s0 = (rest[i : i + PARTS] for i in range(0, 6 * PARTS, PARTS))
    fin = rest[6 * PARTS]
    wsem, ex_s, ex_r, ag_s, ag_r, dd_s, dd_r, pr_s, pr_r, rs_s, rs_r, fin_s, fin_r = rest[6 * PARTS + 1 :]
    wide = half + LANES
    experts = wg_hbm.shape[0]
    hidden_width = wg_hbm.shape[2]
    c, g, d = lax.axis_index("sect"), lax.axis_index("grp"), lax.axis_index("dev")
    other = 1 - c
    me = (g // 2, d % SIDE, (g % 2) * 2 + d // SIDE)

    def device(pos, core):
        x, y, z = pos
        return {"sect": core, "grp": x * 2 + z // 2, "dev": (z % 2) * SIDE + y}

    def shifted(axis, by):
        return tuple(lax.rem(m + by, SIDE) if a == axis else m for a, m in enumerate(me))

    twin = device(me, other)
    right = [device(shifted(a, 1), c) for a in range(3)]
    left = [device(shifted(a, SIDE - 1), c) for a in range(3)]
    far = [device(shifted(a, 2), c) for a in range(3)]
    toward = {1: right, 2: far, 3: left}
    cross = {by: [device(shifted(a, by), other) for a in range(3)] for by in (1, 2, 3)}

    barrier = pltpu.get_barrier_semaphore()
    for peer in [twin] + right + left + far + cross[1] + cross[2] + cross[3]:
        pl.semaphore_signal(barrier, inc=1, device_id=peer, device_id_type=MESH)

    weights = []
    for j in range(experts):
        for i, src in enumerate((wg_hbm, wu_hbm)):
            at = (2 * j + i) * hidden_width
            for h in range(2):
              weights.append(
                pltpu.make_async_copy(src.at[j, h * half : (h + 1) * half], wall.at[h, :, at : at + hidden_width], wsem.at[h, 2 * j + i])
            )
    for j in range(experts):
        for h in range(2):
            weights.append(
                pltpu.make_async_copy(
                    wd_hbm.at[j, :, h * half : (h + 1) * half],
                    wd.at[h, j * hidden_width : (j + 1) * hidden_width],
                    wsem.at[h, 2 * experts + j],
                )
            )
    for copy in weights:
        copy.start()
    lane = lax.broadcasted_iota(jnp.int32, (4, LANES), 1)
    share = jnp.zeros((4, LANES), jnp.float32)
    for k in range(ids.shape[1]):
        share += jnp.where((lane & 31) == ids[:, k : k + 1], shares[:, k : k + 1], 0.0)
    upper = share.astype(jnp.bfloat16).astype(jnp.float32)
    middle = (share - upper).astype(jnp.bfloat16).astype(jnp.float32)
    lower = share - upper - middle
    extra = jnp.where(lane < 32, upper, jnp.where(lane < 64, middle, jnp.where(lane < 96, lower, 0.0)))
    for h in range(2):
        for low, high, value in (
            (0, half, tokens[:, h * half : (h + 1) * half].astype(jnp.float32)),
            (half, wide, extra),
        ):
            eight = jnp.concatenate([value, value], axis=0)
            owner = lax.broadcasted_iota(jnp.int32, eight.shape, 0) // 4
            t8[h, :, low:high] = jnp.where(owner == c, eight, 0.0).astype(jnp.bfloat16)
    pl.semaphore_wait(barrier, 19)

    def remote(src, dst, send, recv, peer):
        return pltpu.make_async_remote_copy(
            src_ref=src, dst_ref=dst, send_sem=send, recv_sem=recv, device_id=peer, device_id_type=MESH
        )

    def spot(part, stage, value):
        order = ORDERS[part]
        index = []
        for axis in range(3):
            if axis in order[:stage]:
                index.append(slice(None))
            elif axis == order[stage]:
                index.append(value)
            else:
                index.append(me[axis])
        return tuple(index) + (slice(None),)

    sent = []

    def go(copy):
        copy.start()
        sent.append(copy)

    swap = remote(t8.at[other], tr, ex_s, ex_r, twin)
    swap.start()
    swap.wait()
    xs[(c,) + me] = t8[c] + tr[...]

    slab = SIDE * SIDE * 8
    ag_parts = split(GATHER)
    steps = (1, SIDE - 1, 2)

    def block(core_half, part, stage, value):
        low, _, high = ag_parts[part]
        return xs.at[(core_half,) + spot(part, stage, value) + (slice(low, high),)]

    def line(core_half, part, second, third):
        low, _, high = ag_parts[part]
        index = [slice(None)] * 3
        index[ORDERS[part][1]] = second
        index[ORDERS[part][2]] = third
        return xs.at[(core_half,) + tuple(index) + (slice(None), slice(low, high))]

    def coord(part, stage, by):
        axis = ORDERS[part][stage]
        return shifted(axis, by)[axis]

    def ag(part, slot, ref, peer):
        return remote(ref, ref, ag_s.at[part, slot], ag_r.at[part, slot], peer)

    def across(part, slot, ref):
        return remote(ref, ref, dd_s.at[part, slot], dd_r.at[part, slot], twin)

    def halved(part, sub, third):
        low, cut, high = ag_parts[part]
        cols = slice(low, cut) if sub == 0 else slice(cut, high)
        return xs.at[(c,) + spot(part, 2, third) + (cols,)]

    def pieces(core_half, part, *thirds):
        low, _, high = ag_parts[part]
        high = min(high, half)
        spots = [spot(part, 2, third) for third in thirds]
        values = [xs[(core_half,) + at + (slice(low, high),)].reshape(slab, high - low) for at in spots]
        value = values[0] if len(values) == 1 else jnp.concatenate(values, axis=0)
        for start in range(0, acc.shape[-1], TILE):
            got = jnp.dot(value, wall[core_half, low:high, start : start + TILE], preferred_element_type=jnp.float32)
            for i, at in enumerate(spots):
                mine = got[i * slab : (i + 1) * slab].reshape(SIDE, SIDE, 8, TILE)
                acc[at + (slice(start, start + TILE),)] += mine

    def first_hop(part):
        ref = block(c, part, 0, coord(part, 0, 0))
        for k, by in enumerate(steps):
            go(ag(part, k, ref, toward[by][ORDERS[part][0]]))

    def second_hop(part):
        for k, by in enumerate(steps):
            ag(part, k, block(c, part, 0, coord(part, 0, SIDE - by)), twin).wait_recv()
        ref = line(c, part, coord(part, 1, 0), coord(part, 2, 0))
        for k, by in enumerate(steps):
            go(ag(part, 3 + k, ref, toward[by][ORDERS[part][1]]))

    def third_hop(part, row):
        by = (0,) + steps
        ref = line(c, part, coord(part, 1, SIDE - by[row]), coord(part, 2, 0))
        if row:
            ag(part, 2 + row, ref, twin).wait_recv()
        go(ag(part, 6 + row, ref, right[ORDERS[part][2]]))
        go(ag(part, 10 + row, ref, left[ORDERS[part][2]]))
        if row == 3:
            go(across(part, 0, block(c, part, 2, coord(part, 2, 0))))

    def fourth_hop(part):
        axis = ORDERS[part][2]
        before, after = coord(part, 2, SIDE - 1), coord(part, 2, 1)
        for third, slot, sub, peer in ((before, 6, 0, right[axis]), (after, 10, 1, left[axis])):
            for row, by in enumerate((0,) + steps):
                ag(part, slot + row, line(c, part, coord(part, 1, SIDE - by), third), twin).wait_recv()
            go(ag(part, 14 + sub, halved(part, sub, third), peer))
        go(across(part, 1, block(c, part, 2, before)))
        go(across(part, 2, block(c, part, 2, after)))

    def last_hop(part):
        opposite = coord(part, 2, 2)
        ag(part, 14, halved(part, 0, opposite), twin).wait_recv()
        ag(part, 15, halved(part, 1, opposite), twin).wait_recv()
        go(across(part, 3, block(c, part, 2, opposite)))

    def arrived(part, slot):
        value = coord(part, 2, (0, SIDE - 1, 1, 2)[slot])
        across(part, slot, block(other, part, 2, value)).wait_recv()

    def near(core_half, wave):
        for part in wave:
            if core_half is other:
                arrived(part, 0)
            pieces(core_half, part, coord(part, 2, 0))

    def beside(core_half, wave):
        for part in wave:
            if core_half is other:
                arrived(part, 1)
                arrived(part, 2)
            pieces(core_half, part, coord(part, 2, 1), coord(part, 2, SIDE - 1))

    def opposite(core_half, wave):
        for part in wave:
            if core_half is other:
                arrived(part, 3)
            pieces(core_half, part, coord(part, 2, 2))

    def each(step, wave):
        for part in wave:
            step(part)

    for wave in WAVES:
        each(first_hop, wave)
    acc[...] = jnp.zeros_like(acc)
    for wave in WAVES:
        each(second_hop, wave)
        for part in wave:
            third_hop(part, 0)
    for wave in WAVES:
        for row in range(1, SIDE):
            for part in wave:
                third_hop(part, row)
    for copy in weights:
        copy.wait()
    w0, w1, w2 = WAVES
    near(c, w0)
    near(c, w1)
    each(fourth_hop, w0)
    near(c, w2)
    near(other, w0)
    near(other, w1)
    each(fourth_hop, w1)
    near(other, w2)
    beside(c, w0)
    each(fourth_hop, w2)
    beside(other, w0)
    each(last_hop, w0)
    beside(c, w1)
    beside(other, w1)
    each(last_hop, w1)
    beside(c, w2)
    opposite(c, w0)
    each(last_hop, w2)
    beside(other, w2)
    opposite(other, w0)
    opposite(c, w1)
    opposite(other, w1)
    opposite(c, w2)
    opposite(other, w2)

    first = (c * 8 + g) * experts
    row = lax.broadcasted_iota(jnp.int32, (LANES, hidden_width), 0)
    picks = []
    for j in range(experts):
        e = first + j
        hit = (row == e) | (row == e + 32) | (row == e + 64)
        picks.append(jnp.where(hit, 1.0, 0.0).astype(jnp.bfloat16))
    def act_step(i, carry):
        share = xs[0, i, :, :, :, half:wide].reshape(slab, LANES)
        for j in range(experts):
            at = 2 * j * hidden_width
            gate = acc[i, :, :, :, at : at + hidden_width].reshape(slab, hidden_width)
            up = acc[i, :, :, :, at + hidden_width : at + 2 * hidden_width].reshape(slab, hidden_width)
            weight = jnp.dot(share, picks[j], preferred_element_type=jnp.float32)
            act = gate / (1.0 + jnp.exp(-gate)) * up * weight
            hid[pl.ds(pl.multiple_of(i * slab, slab), slab), j * hidden_width : (j + 1) * hidden_width] = act.astype(
                jnp.bfloat16
            )
        return carry

    lax.fori_loop(0, SIDE, act_step, 0)

    rs_parts = split(SCATTER)

    def down(half_index, part, add):
        low, _, high = rs_parts[part]

        value = hid[...]
        for start in range(low, high, TILE):
            stop = min(start + TILE, high)
            at = (slice(None),) * 4 + (slice(start, stop),)
            got = jnp.dot(value, wd[half_index, :, start:stop], preferred_element_type=jnp.float32)
            if add:
                got += r0[at].reshape(got.shape).astype(jnp.float32)
            ps[(half_index,) + at] = got.astype(jnp.bfloat16).reshape(SIDE, SIDE, SIDE, 8, stop - start)

    def pair(half_index, part):
        low, _, high = rs_parts[part]
        cols = (slice(None),) * 4 + (slice(low, high),)
        return remote(ps.at[(half_index,) + cols], r0.at[cols], pr_s.at[part], pr_r.at[part], twin)

    def plus(index, *others):
        total = ps[index].astype(jnp.float32)
        for value in others:
            total += value.astype(jnp.float32)
        ps[index] = total.astype(jnp.bfloat16)

    def big(part, kind):
        axis = ORDERS[part][2]
        low, cut, high = rs_parts[part]
        by, start, stop, buf, peer = (
            (2, low, cut, fa, right),
            (2, cut, high, fb, left),
            (1, cut, high, rl, right),
            (SIDE - 1, low, cut, rr, left),
            (1, low, cut, rl, right),
            (SIDE - 1, cut, high, rr, left),
        )[kind]
        ref = ps.at[(c,) + spot(part, 2, shifted(axis, by)[axis]) + (slice(start, stop),)]
        dst = buf[part]
        if kind > 1:
            dst = dst.at[:, :, :, start - low : stop - low]
        return remote(ref, dst, rs_s.at[part, kind], rs_r.at[part, kind], peer[axis])

    def small(part, stage, k):
        axis = ORDERS[part][stage]
        low, _, high = rs_parts[part]
        ref = ps.at[(c,) + spot(part, stage, shifted(axis, steps[k])[axis]) + (slice(low, high),)]
        dst = (s0, s1)[stage][part].at[k]
        return remote(
            ref, dst, rs_s.at[part, 6 + 3 * stage + k], rs_r.at[part, 6 + 3 * stage + k], toward[steps[k]][axis]
        )

    def swapped(part, k):
        axis = ORDERS[part][0]
        low, _, high = rs_parts[part]
        peer = cross[steps[k]][axis] if k < 3 else twin
        by = steps[k] if k < 3 else 0
        ref = ps.at[(c,) + spot(part, 0, shifted(axis, by)[axis]) + (slice(low, high),)]
        return remote(ref, fin.at[k, :, low:high], fin_s.at[part, k], fin_r.at[part, k], peer)

    def accumulate(part, by, low, high, others):
        axis = ORDERS[part][2]
        base = rs_parts[part][0]
        index = (c,) + spot(part, 2, shifted(axis, by)[axis]) + (slice(low, high),)
        free = [i for i, s in enumerate(index[:-2]) if isinstance(s, slice)][0]

        def step(i, carry):
            inner = tuple(i if k == free else s for k, s in enumerate(index))
            plus(inner, *[o[i, :, :, at : at + high - low] for o, at in others])
            return carry

        lax.fori_loop(0, SIDE, step, 0)

    def forward(part):
        low, cut, high = rs_parts[part]
        big(part, 0).wait_recv()
        accumulate(part, 1, low, cut, [(fa[part], 0)])
        go(big(part, 4))
        big(part, 1).wait_recv()
        accumulate(part, SIDE - 1, cut, high, [(fb[part], 0)])
        go(big(part, 5))

    def settle(part):
        low, cut, high = rs_parts[part]
        for kind in range(2, 6):
            big(part, kind).wait_recv()
        accumulate(part, 0, low, high, [(rl[part], 0), (rr[part], 0)])
        for k in range(3):
            go(small(part, 1, k))

    def finish_axis(part, stage):
        low, cut, high = rs_parts[part]
        for k in range(3):
            small(part, stage, k).wait_recv()
        index = (c,) + spot(part, stage, me[ORDERS[part][stage]]) + (slice(low, high),)
        if stage == 0:
            total = ps[index].astype(jnp.float32)
            for k in range(3):
                total += s0[part][k].astype(jnp.float32)
            out[:, pl.ds(pl.multiple_of(c * half + low, LANES), high - low)] = total.astype(jnp.bfloat16)
            total = jnp.zeros((8, high - low), jnp.float32)
            for k in range(4):
                swapped(part, k).wait_recv()
                total += fin[k, :, low:high].astype(jnp.float32)
            out[:, pl.ds(pl.multiple_of(other * half + low, LANES), high - low)] = total.astype(jnp.bfloat16)
            return
        plus(index, *[s1[part][k] for k in range(3)])
        if stage:
            for k in range(3):
                go(small(part, 0, k))
                go(swapped(part, k))
            go(swapped(part, 3))

    for part in range(AHEAD):
        down(other, part, False)
        go(pair(other, part))
    for part in range(PARTS):
        if part + AHEAD < PARTS:
            down(other, part + AHEAD, False)
            go(pair(other, part + AHEAD))
        pair(c, part).wait_recv()
        down(c, part, True)
        for kind in range(4):
            go(big(part, kind))
        if part >= LAG:
            forward(part - LAG)
    for part in range(PARTS - LAG, PARTS):
        forward(part)
    each(settle, w0)
    each(settle, w1)
    for part in w0:
        finish_axis(part, 1)
    each(settle, w2)
    for part in w1:
        finish_axis(part, 1)
    for part in w0:
        finish_axis(part, 0)
    for part in w2:
        finish_axis(part, 1)
    for part in w1:
        finish_axis(part, 0)
    for part in w2:
        finish_axis(part, 0)

    for copy in sent:
        copy.wait_send()


def body(tokens, expert_ids, gate_weights, w_gate, w_up, w_down):
    row_count, model_width = tokens.shape
    half = model_width // 2
    experts, _, hidden_width = w_gate.shape
    c = lax.axis_index("sect")
    wide = half + LANES
    sides = (SIDE,) * 3
    bf16 = jnp.bfloat16
    rs_parts = split(SCATTER)
    plane = (SIDE, SIDE, 8)
    landing = [plane + (cut - lo,) for lo, cut, hi in rs_parts]
    landing += [plane + (hi - cut,) for lo, cut, hi in rs_parts]
    landing += [plane + (hi - lo,) for lo, cut, hi in rs_parts] * 2
    landing += [(3, SIDE, 8, hi - lo) for lo, cut, hi in rs_parts]
    landing += [(3, 8, hi - lo) for lo, cut, hi in rs_parts]
    scratch = [
        pltpu.VMEM((2, 8, wide), bf16),
        pltpu.VMEM((8, wide), bf16),
        pltpu.VMEM((2,) + sides + (8, wide), bf16),
        pltpu.VMEM((2, half, 2 * experts * hidden_width), bf16),
        pltpu.VMEM((2, experts * hidden_width, half), bf16),
        pltpu.VMEM(sides + (8, 2 * experts * hidden_width), jnp.float32),
        pltpu.VMEM((8 * SIDE**3, experts * hidden_width), bf16),
        pltpu.VMEM((2,) + sides + (8, half), bf16),
        pltpu.VMEM(sides + (8, half), bf16),
    ]
    scratch += [pltpu.VMEM(s, bf16) for s in landing]
    scratch += [pltpu.VMEM((4, 8, half), bf16)]
    dma = pltpu.SemaphoreType.DMA
    scratch += [
        dma((2, 3 * experts)),
        dma,
        dma,
        dma((PARTS, 16)),
        dma((PARTS, 16)),
        dma((PARTS, 4)),
        dma((PARTS, 4)),
        dma((PARTS,)),
        dma((PARTS,)),
        dma((PARTS, 12)),
        dma((PARTS, 12)),
        dma((PARTS, 4)),
        dma((PARTS, 4)),
    ]
    anywhere = pl.BlockSpec(memory_space=pl.ANY)
    vmem = pl.BlockSpec(memory_space=pltpu.VMEM)
    out = pl.pallas_call(
        functools.partial(kernel, half),
        out_shape=jax.ShapeDtypeStruct((8, model_width), bf16),
        in_specs=[vmem, vmem, vmem, anywhere, anywhere, anywhere],
        out_specs=vmem,
        scratch_shapes=scratch,
        compiler_params=pltpu.CompilerParams(
            collective_id=0, has_side_effects=True, vmem_limit_bytes=60 * 1024 * 1024
        ),
    )(tokens, expert_ids, gate_weights, w_gate, w_up, w_down)
    return lax.dynamic_slice_in_dim(out, c * row_count, row_count, axis=0)


def solution(mesh):
    in_specs = (
        P(ALL, None),
        P(ALL, None),
        P(ALL, None),
        P(("sect", "grp"), None, "dev"),
        P(("sect", "grp"), None, "dev"),
        P(("sect", "grp"), "dev", None),
    )
    return jax.shard_map(body, mesh=mesh, in_specs=in_specs, out_specs=P(ALL, None), check_vma=False)
```
